32 devices in a mesh: seq: 4 (over y, core), batch: 8 (over z, x).
Axes of the slice: x: 2, y: 2, z: 4, core: 2. Of those that a mesh axis runs over, the one named last changes fastest.
Arguments:
- waveforms: bfloat16 [8, 24, 16000], P('batch', 'seq'), may hold values from -6 to 6
- clip_lengths: int32 [8, 4], P('batch'), may hold values from 1 to 6, as said below
- block_starts: int32 [8, 24], P('batch'), may hold values from 0 to 744, as said below
- conv_first: bfloat16 [384, 1280], P('batch'), may hold values from -0.3125 to 0.3125
- bias_first: float32 [1280], replicated, may hold values from -3 to 3
- conv_second: bfloat16 [3840, 1280], replicated, may hold values from -0.09375 to 0.09375
- bias_second: float32 [1280], replicated, may hold values from -3 to 3
- norm_gain: float32 [1280], replicated, may hold values from 0.25 to 1.75
- projector: bfloat16 [1280, 4096], P(None, 'seq'), may hold values from -0.15625 to 0.15625
- proj_bias: float32 [4096], P('seq'), may hold values from -3 to 3
Outputs:
- audio_rows: bfloat16 [8, 768, 4096], P('batch', 'seq')
The draws below stay inside these ranges and needn't reach their ends.
Inputs may be any that keep to these rules, and one draw needn't show every extreme that they name: `clip_lengths`: the lengths of a sequence's 4 clips sum to 12, and one clip has 6 blocks. `block_starts`: A clip's live blocks start 24 positions apart, in slot order; live blocks of a sequence occupy disjoint positions; entries of dead slots are 0.
All inputs are finite; a program needn't handle non-finite values.
Results may differ from the reference program's by a relative error of at most 0.0055.
Values may be sent and summed in bfloat16 or wider, within the bound.
A program may use at most 64 MiB of HBM per device.

```python
import jax
import jax.numpy as jnp
import numpy as np
from jax import lax

MEL = 128
WIDTH = 1280
DMODEL = 4096
HOP = 160
WINDOW = 400
BINS = 201
FRAMES = 96
TOK = 24
SAMPLES = 16000
W = 3
SLOTS = 6
OWN_ROWS = 192
LENGTH = 768
GROUPS = 8
N_SEQ = 4


def group_plan(key):
    key_list = jax.random.split(key, 4)
    order_dev = jax.random.permutation(key_list[0], N_SEQ)
    amplitudes = jax.random.randint(key_list[1], (N_SEQ,), 0, W)
    position = jnp.arange(N_SEQ)
    offset_pos = position - 3
    pair_index = jnp.maximum(offset_pos, 0) // 2
    sign_of = jnp.where(offset_pos % 2 == 0, 1, -1)
    delta = sign_of * amplitudes[pair_index]
    delta = jnp.where((offset_pos % 2 == 0) & (position == N_SEQ - 1), 0, delta)
    delta = jnp.where(position == 2, -(W - W // 2), delta)
    delta = jnp.where(position == 1, -(W // 2), delta)
    delta = jnp.where(position == 0, W, delta)
    lengths = jnp.zeros((N_SEQ,), jnp.int32).at[order_dev].set((W + delta).astype(jnp.int32))
    clip_order = jax.random.permutation(key_list[2], N_SEQ)
    spare = OWN_ROWS - W * TOK
    swings = jax.random.randint(key_list[3], (N_SEQ,), 0, spare + 1)
    other_pos = position - 2
    gap_sizes = spare + jnp.where(other_pos % 2 == 0, 1, -1) * swings[jnp.maximum(other_pos, 0) // 2]
    gap_sizes = jnp.where(position == 1, 2 * spare, gap_sizes)
    gap_sizes = jnp.where(position == 0, 0, gap_sizes)
    clip_rows = TOK * lengths[clip_order]
    clip_begin = jnp.cumsum(gap_sizes + clip_rows) - clip_rows
    device_begin = jnp.zeros((N_SEQ,), jnp.int32).at[clip_order].set(clip_begin.astype(jnp.int32))
    slot_index = jnp.arange(SLOTS)
    starts = jnp.where(slot_index[None, :] < lengths[:, None], device_begin[:, None] + TOK * slot_index[None, :], 0)
    return (lengths, starts.reshape(-1).astype(jnp.int32))


def draw_clip_lengths(key, part):
    key_list = jax.random.split(jax.random.fold_in(key, 11), GROUPS)
    return jax.vmap(group_plan)(key_list)[0]


def draw_block_starts(key, part):
    key_list = jax.random.split(jax.random.fold_in(key, 11), GROUPS)
    return jax.vmap(group_plan)(key_list)[1]


def shard_levels(rng, extent, cuts, least, top_value):
    gain = 1.0
    for dim, parts in cuts:
        heights = jax.random.uniform(jax.random.fold_in(jax.random.fold_in(rng, 6), dim), (parts,), jnp.float32, least / len(cuts), top_value / len(cuts))
        gain = gain * jnp.repeat(jnp.exp(heights), extent[dim] // parts).reshape((-1,) + (1,) * (len(extent) - 1 - dim))
    return gain


def noise(own_key, shape, deviation, most, cuts=(), kind=jnp.bfloat16):
    values = jax.random.normal(own_key, shape, jnp.float32) * deviation
    if len(cuts) > 0:
        values = shard_levels(own_key, shape, cuts, -0.22, 0.18) * values
    return jnp.clip(values, min=-most, max=most).astype(kind)


def setup_inputs(seed: int = 0) -> dict:
    splits = jax.random.split(jax.random.key(seed), 11)
    waveforms = noise(splits[0], (GROUPS, N_SEQ * SLOTS, SAMPLES), 1.0, 6.0, ((0, 8), (1, 4)))
    clip_lengths = draw_clip_lengths(jax.random.fold_in(splits[10], 71), 0)
    block_starts = draw_block_starts(jax.random.fold_in(splits[10], 71), 0)
    conv_first = noise(splits[3], (3 * MEL, WIDTH), (3 * MEL) ** -0.5, 0.3125, ((0, 8),))
    bias_first = noise(splits[4], (WIDTH,), 0.5, 3.0, (), jnp.float32)
    conv_second = noise(splits[5], (3 * WIDTH, WIDTH), (3 * WIDTH) ** -0.5, 0.09375)
    bias_second = noise(splits[6], (WIDTH,), 0.5, 3.0, (), jnp.float32)
    norm_gain = jnp.clip(1.0 + 0.15 * jax.random.normal(splits[7], (WIDTH,), jnp.float32), 0.25, 1.75)
    projector = noise(splits[8], (WIDTH, DMODEL), WIDTH ** -0.5, 0.15625, ((1, 4),))
    proj_bias = noise(splits[9], (DMODEL,), 0.5, 3.0, ((0, 4),), jnp.float32)
    return dict(waveforms=waveforms, clip_lengths=clip_lengths, block_starts=block_starts, conv_first=conv_first, bias_first=bias_first, conv_second=conv_second, bias_second=bias_second, norm_gain=norm_gain, projector=projector, proj_bias=proj_bias)


def hertz_to_mel(hertz):
    return np.where(hertz < 1000.0, hertz / (200.0 / 3.0), 15.0 + np.log(np.maximum(hertz, 1.0) / 1000.0) / (np.log(6.4) / 27.0))

def mel_to_hertz(mels):
    return np.where(mels < 15.0, mels * 200.0 / 3.0, 1000.0 * np.exp((mels - 15.0) * np.log(6.4) / 27.0))

def spectral_tables():
    sample_rate = HOP * 100.0
    sample_index = np.arange(WINDOW)
    hann = 0.5 - 0.5 * np.cos(2.0 * np.pi * sample_index / WINDOW)
    angles = 2.0 * np.pi * np.outer(sample_index, np.arange(BINS)) / WINDOW
    dft_basis = np.concatenate([hann[:, None] * np.cos(angles), -hann[:, None] * np.sin(angles)], axis=1)
    edges = mel_to_hertz(np.linspace(0.0, float(hertz_to_mel(np.array(sample_rate / 2.0))), MEL + 2))
    bin_hertz = np.arange(BINS) * sample_rate / WINDOW
    rising = (bin_hertz[:, None] - edges[None, :-2]) / (edges[1:-1] - edges[:-2])[None, :]
    falling = (edges[None, 2:] - bin_hertz[:, None]) / (edges[2:] - edges[1:-1])[None, :]
    filters = np.maximum(0.0, np.minimum(rising, falling)) * (2.0 / (edges[2:] - edges[:-2]))[None, :]
    return (jnp.asarray(dft_basis.astype(np.float32)), jnp.asarray(filters.astype(np.float32)))

def encode(blocks_in, tables, conv_first, bias_first, conv_second, bias_second, norm_gain):
    dft_basis, filters = tables
    block_count = blocks_in.shape[0]
    segments = blocks_in.astype(jnp.float32).reshape(block_count, FRAMES + 4, HOP)
    frames = jnp.concatenate([segments[:, :FRAMES], segments[:, 1:FRAMES + 1], segments[:, 2:FRAMES + 2, :HOP // 2]], axis=2)
    frames = frames.reshape(block_count * FRAMES, WINDOW)
    spectrum = jnp.dot(frames, dft_basis, precision=lax.Precision.HIGHEST)
    power_bins = spectrum[:, :BINS] * spectrum[:, :BINS] + spectrum[:, BINS:] * spectrum[:, BINS:]
    energy = jnp.dot(power_bins, filters, precision=lax.Precision.HIGHEST)
    features = ((jnp.log10(energy + 1e-10) + 4.0) / 4.0).astype(jnp.bfloat16).reshape(block_count, FRAMES, MEL)
    zero_mel = jnp.zeros((block_count, 1, MEL), jnp.bfloat16)
    padded = jnp.concatenate([zero_mel, features, zero_mel], axis=1)
    stacked = jnp.concatenate([padded[:, :-2], padded[:, 1:-1], padded[:, 2:]], axis=2).reshape(block_count * FRAMES, 3 * MEL)
    hidden = jax.nn.gelu(jnp.dot(stacked, conv_first, preferred_element_type=jnp.float32) + bias_first, approximate=False)
    hidden = hidden.astype(jnp.bfloat16).reshape(block_count, FRAMES // 2, 2, WIDTH)
    even_rows = hidden[:, :, 0]
    odd_rows = hidden[:, :, 1]
    before = jnp.concatenate([jnp.zeros((block_count, 1, WIDTH), jnp.bfloat16), odd_rows[:, :-1]], axis=1)
    second_in = jnp.concatenate([before, even_rows, odd_rows], axis=2).reshape(block_count * FRAMES // 2, 3 * WIDTH)
    activated = jax.nn.gelu(jnp.dot(second_in, conv_second, preferred_element_type=jnp.float32) + bias_second, approximate=False)
    pooled = lax.optimization_barrier(jnp.mean(activated.reshape(block_count, TOK, 2, WIDTH), axis=2))
    row_mean = lax.optimization_barrier(jnp.mean(pooled, axis=-1, keepdims=True))
    centred = pooled - row_mean
    row_var = lax.optimization_barrier(jnp.mean(centred * centred, axis=-1, keepdims=True))
    normed = centred / jnp.sqrt(row_var + 1e-05) * norm_gain
    return normed.astype(jnp.bfloat16).reshape(block_count * TOK, WIDTH)

def reference(waveforms, clip_lengths, block_starts, conv_first, bias_first, conv_second, bias_second, norm_gain, projector, proj_bias):
    tables = spectral_tables()

    def one_group(inputs):
        group_waves, group_lengths, group_starts = inputs
        token_rows = encode(group_waves, tables, conv_first, bias_first, conv_second, bias_second, norm_gain)
        projected = (jnp.dot(token_rows, projector, preferred_element_type=jnp.float32) + proj_bias).astype(jnp.bfloat16)
        slot_index = (jnp.arange(N_SEQ * SLOTS) % SLOTS).astype(jnp.int32)
        is_live = slot_index < jnp.repeat(group_lengths, SLOTS).astype(jnp.int32)
        offsets = jnp.arange(TOK).astype(jnp.int32)
        target = jnp.where(is_live[:, None], group_starts.astype(jnp.int32)[:, None] + offsets[None, :], LENGTH).reshape(-1)
        return jnp.zeros((LENGTH, DMODEL), jnp.bfloat16).at[target].set(projected, mode='drop')
    return lax.map(one_group, (waveforms, clip_lengths, block_starts))
```

```python
import functools

import jax
import jax.numpy as jnp
import ml_dtypes
import numpy as np
from jax import lax
from jax.experimental import pallas as pl
from jax.experimental.pallas import tpu as pltpu
from jax.sharding import PartitionSpec as P

MEL = 128
WIDTH = 1280
HOP = 160
WINDOW = 400
BINS = 201
TOK = 24
OWN_ROWS = 192
W = 3
ROWS = W * TOK
HALF = WIDTH // 2
CHUNK = 256
SEGS = 25
SEG = 4 * HOP
PIECES = 2
MESH = pl.DeviceIdType.MESH


def hertz_to_mel(hertz):
    return np.where(
        hertz < 1000.0,
        hertz / (200.0 / 3.0),
        15.0 + np.log(np.maximum(hertz, 1.0) / 1000.0) / (np.log(6.4) / 27.0),
    )


def mel_to_hertz(mels):
    return np.where(
        mels < 15.0, mels * 200.0 / 3.0, 1000.0 * np.exp((mels - 15.0) * np.log(6.4) / 27.0)
    )


def spectral_tables():
    sample_rate = HOP * 100.0
    sample_index = np.arange(WINDOW)
    hann = 0.5 - 0.5 * np.cos(2.0 * np.pi * sample_index / WINDOW)
    angles = 2.0 * np.pi * np.outer(sample_index, np.arange(BINS)) / WINDOW
    basis = np.zeros((512, 512), np.float32)
    basis[:WINDOW, :BINS] = hann[:, None] * np.cos(angles)
    basis[:WINDOW, 256 : 256 + BINS] = -hann[:, None] * np.sin(angles)
    edges = mel_to_hertz(
        np.linspace(0.0, float(hertz_to_mel(np.array(sample_rate / 2.0))), MEL + 2)
    )
    bin_hertz = np.arange(BINS) * sample_rate / WINDOW
    rising = (bin_hertz[:, None] - edges[None, :-2]) / (edges[1:-1] - edges[:-2])[None, :]
    falling = (edges[None, 2:] - bin_hertz[:, None]) / (edges[2:] - edges[1:-1])[None, :]
    filters = np.zeros((256, MEL), np.float32)
    filters[:BINS] = (
        np.maximum(0.0, np.minimum(rising, falling)) * (2.0 / (edges[2:] - edges[:-2]))[None, :]
    )
    terms = []
    rest = basis
    for _ in range(3):
        term = rest.astype(ml_dtypes.bfloat16)
        terms.append(term)
        rest = rest - term.astype(np.float32)
    return jnp.asarray(np.stack(terms)), jnp.asarray(filters)


def gelu(x):
    return 0.5 * x * (1.0 + lax.erf(x * np.float32(np.sqrt(0.5))))


def shift_rows(x, by):
    rows = x.shape[0]
    moved = pltpu.roll(x, by % rows, axis=0)
    place = lax.broadcasted_iota(jnp.int32, (rows, 1), 0) % TOK
    edge = 0 if by == 1 else TOK - 1
    return jnp.where(place == edge, 0.0, moved)


def kernel(
    n_seq,
    n_batch,
    slots,
    lengths_ref,
    starts_ref,
    waves_hbm,
    first_hbm,
    bias1_ref,
    second_hbm,
    bias2_ref,
    gain_ref,
    projector_hbm,
    pbias_ref,
    basis_hbm,
    filters_ref,
    out_ref,
    waves,
    first,
    second,
    projector,
    basis,
    conv_in,
    pooled,
    tokens,
    placed,
    local_sem,
    wave_send,
    wave_recv,
    first_send,
    first_recv,
    tok_send,
    tok_recv,
    out_send,
    out_recv,
):
    me = lax.axis_index("seq")
    row = lax.axis_index("batch")
    core = lax.rem(me, 2)
    chip = lax.div(me, 2)
    n_chip = n_seq // 2
    partner = chip * 2 + (1 - core)
    cols = projector.shape[1]
    piece = cols // PIECES

    def across(k):
        return lax.rem(chip + k, n_chip) * 2 + core

    def source(k):
        return lax.rem(chip - k + n_chip, n_chip) * 2 + core

    def peer(k):
        return lax.rem(row + k, n_batch)

    loads = [
        pltpu.make_async_copy(waves_hbm, waves.at[pl.ds(me * slots, slots)], local_sem.at[0]),
        pltpu.make_async_copy(basis_hbm, basis, local_sem.at[1]),
        pltpu.make_async_copy(first_hbm, first.at[row], local_sem.at[2]),
        pltpu.make_async_copy(second_hbm, second, local_sem.at[3]),
        pltpu.make_async_copy(projector_hbm, projector, local_sem.at[4]),
    ]
    for load in loads:
        load.start()

    barrier = pltpu.get_barrier_semaphore()
    pl.semaphore_signal(barrier, inc=1, device_id=(partner, row), device_id_type=MESH)
    for k in range(1, n_chip):
        pl.semaphore_signal(barrier, inc=1, device_id=(across(k), row), device_id_type=MESH)
    for k in range(1, n_batch):
        pl.semaphore_signal(barrier, inc=1, device_id=(me, peer(k)), device_id_type=MESH)
    pl.semaphore_wait(barrier, n_chip + n_batch - 1)

    def gather(own, place, send, recv):
        copies = []
        for k in range(n_chip):
            target = partner if k == 0 else across(k)
            copies.append(
                pltpu.make_async_remote_copy(
                    src_ref=own,
                    dst_ref=place(me),
                    send_sem=send.at[k],
                    recv_sem=recv.at[k],
                    device_id=(target, row),
                    device_id_type=MESH,
                )
            )
        return copies

    def relay(place, send, recv):
        return [
            pltpu.make_async_remote_copy(
                src_ref=place(source(k)),
                dst_ref=place(source(k)),
                send_sem=send.at[n_chip - 1 + k],
                recv_sem=recv.at[n_chip - 1 + k],
                device_id=(partner, row),
                device_id_type=MESH,
            )
            for k in range(1, n_chip)
        ]

    def wave_place(s):
        return waves.at[pl.ds(s * slots, slots)]

    wave_copies = gather(waves_hbm, wave_place, wave_send, wave_recv)
    wave_relays = relay(wave_place, wave_send, wave_recv)
    for copy in wave_copies[1:] + wave_copies[:1]:
        copy.start()

    half = pl.ds(pl.multiple_of(core * HALF, 128), HALF)
    first_copies = []
    first_relays = []
    for k in range(1, n_batch):
        first_copies.append(
            pltpu.make_async_remote_copy(
                src_ref=first_hbm.at[:, half],
                dst_ref=first.at[row, :, half],
                send_sem=first_send.at[k - 1],
                recv_sem=first_recv.at[k - 1],
                device_id=(me, peer(k)),
                device_id_type=MESH,
            )
        )
        origin = lax.rem(row - k + n_batch, n_batch)
        first_relays.append(
            pltpu.make_async_remote_copy(
                src_ref=first.at[origin, :, half],
                dst_ref=first.at[origin, :, half],
                send_sem=first_send.at[n_batch - 2 + k],
                recv_sem=first_recv.at[n_batch - 2 + k],
                device_id=(partner, row),
                device_id_type=MESH,
            )
        )
    for copy in first_copies:
        copy.start()

    for k in range(1, n_chip):
        wave_copies[k].wait_recv()
        wave_relays[k - 1].start()
    wave_copies[0].wait_recv()
    for copy in wave_relays:
        copy.wait_recv()
    loads[0].wait()

    ends = []
    total = 0
    for d in range(n_seq):
        total = total + lengths_ref[0, d]
        ends.append(total)

    def live_slot(j):
        slot = j
        for d in range(n_seq - 1):
            slot = slot + jnp.where(j >= ends[d], slots - lengths_ref[0, d], 0)
        return jnp.clip(slot, 0, n_seq * slots - 1)

    pieces = []
    for i in range(W):
        block = waves[live_slot(me * W + i)].astype(jnp.float32)
        pieces.append(jnp.concatenate([block[: SEGS - 1], block[1:, :256]], axis=1))
    samples = jnp.concatenate(pieces, axis=0)
    frames = [samples[:, :512]]
    for r in range(1, 4):
        wide = samples[:, 128 * r : min(128 * r + 640, 896)]
        frames.append(pltpu.roll(wide, wide.shape[1] - 32 * r, axis=1)[:, :512])
    frames = jnp.concatenate(frames, axis=0).astype(jnp.bfloat16)
    loads[1].wait()
    spectrum = jnp.dot(frames, basis[2], preferred_element_type=jnp.float32)
    spectrum += jnp.dot(frames, basis[1], preferred_element_type=jnp.float32)
    spectrum += jnp.dot(frames, basis[0], preferred_element_type=jnp.float32)
    real, imag = spectrum[:, :256], spectrum[:, 256:]
    power = real * real + imag * imag
    energy = jnp.dot(
        power,
        filters_ref[...],
        precision=lax.Precision.HIGHEST,
        preferred_element_type=jnp.float32,
    )
    features = (jnp.log(energy + 1e-10) * np.float32(1.0 / np.log(10.0)) + 4.0) * 0.25
    feat = [features[r * ROWS : (r + 1) * ROWS] for r in range(4)]
    stacked = jnp.concatenate(
        [
            jnp.concatenate([shift_rows(feat[3], 1)] + feat[:3], axis=0),
            features,
            jnp.concatenate(feat[1:] + [shift_rows(feat[0], -1)], axis=0),
        ],
        axis=1,
    ).astype(jnp.bfloat16)

    for k in range(n_batch - 1):
        first_copies[k].wait_recv()
        first_relays[k].start()
    for copy in first_relays:
        copy.wait_recv()
    loads[2].wait()

    @pl.loop(0, WIDTH // CHUNK)
    def _(n):
        at = pl.ds(pl.multiple_of(n * CHUNK, CHUNK), CHUNK)
        weight = first[:, :, at].reshape(3 * MEL, CHUNK)
        hidden = gelu(
            jnp.dot(stacked, weight, preferred_element_type=jnp.float32) + bias1_ref[:, at]
        )
        hid = [hidden[r * ROWS : (r + 1) * ROWS] for r in range(4)]
        taps = [[shift_rows(hid[3], 1), hid[1]], [hid[0], hid[2]], [hid[1], hid[3]]]
        for t in range(3):
            to = pl.ds(pl.multiple_of(t * WIDTH + n * CHUNK, CHUNK), CHUNK)
            conv_in[:, to] = jnp.concatenate(taps[t], axis=0).astype(jnp.bfloat16)

    loads[3].wait()

    @pl.loop(0, WIDTH // CHUNK)
    def _(n):
        at = pl.ds(pl.multiple_of(n * CHUNK, CHUNK), CHUNK)
        activated = gelu(
            jnp.dot(conv_in[...], second[:, at], preferred_element_type=jnp.float32)
            + bias2_ref[:, at]
        )
        pooled[:, at] = (activated[:ROWS] + activated[ROWS:]) * 0.5

    whole = pooled[...]
    centred = whole - jnp.mean(whole, axis=1, keepdims=True)
    variance = jnp.mean(centred * centred, axis=1, keepdims=True)
    normed = centred / jnp.sqrt(variance + 1e-05) * gain_ref[...]
    tokens[me] = jnp.concatenate([normed[:, :HALF], normed[:, HALF:]], axis=0).astype(jnp.bfloat16)

    def tok_place(s):
        return tokens.at[s]

    tok_copies = gather(tokens.at[me], tok_place, tok_send, tok_recv)
    tok_relays = relay(tok_place, tok_send, tok_recv)
    for copy in tok_copies[1:] + tok_copies[:1]:
        copy.start()
    tok_copies[0].wait_recv()
    loads[4].wait()

    def group_rows(g):
        pair = [tokens[g * 2 + c].astype(jnp.float32) for c in range(2)]
        left = jnp.concatenate([p[:ROWS] for p in pair], axis=0).astype(jnp.bfloat16)
        right = jnp.concatenate([p[ROWS:] for p in pair], axis=0).astype(jnp.bfloat16)
        return left, right

    out_copies = []
    out_relays = []
    for k in range(n_chip):
        g = lax.rem(chip - k + n_chip, n_chip)
        if k > 0:
            tok_copies[k].wait_recv()
            tok_relays[k - 1].start()
            tok_relays[k - 1].wait_recv()
        left, right = group_rows(g)
        for h in range(PIECES):
            at = slice(h * piece, (h + 1) * piece)
            value = jnp.dot(left, projector[:HALF, at], preferred_element_type=jnp.float32)
            value += jnp.dot(right, projector[HALF:, at], preferred_element_type=jnp.float32)
            placed[k, h, me] = (value + pbias_ref[:, at]).astype(jnp.bfloat16)

            step = []
            for j in range(n_chip):
                target = partner if j == 0 else across(j)
                step.append(
                    pltpu.make_async_remote_copy(
                        src_ref=placed.at[k, h, me],
                        dst_ref=placed.at[(k + j) % n_chip, h, me],
                        send_sem=out_send.at[k, h, j],
                        recv_sem=out_recv.at[k, h, j],
                        device_id=(target, row),
                        device_id_type=MESH,
                    )
                )
            for copy in step[1:] + step[:1]:
                copy.start()
            out_copies.append((k, h, step))
            out_relays.append(
                [
                    pltpu.make_async_remote_copy(
                        src_ref=placed.at[(k + j) % n_chip, h, source(j)],
                        dst_ref=placed.at[(k + j) % n_chip, h, source(j)],
                        send_sem=out_send.at[k, h, n_chip - 1 + j],
                        recv_sem=out_recv.at[k, h, n_chip - 1 + j],
                        device_id=(partner, row),
                        device_id_type=MESH,
                    )
                    for j in range(1, n_chip)
                ]
            )

    span = 2 * ROWS
    column = lax.broadcasted_iota(jnp.int32, (1, span), 1)
    position = lax.broadcasted_iota(jnp.int32, (OWN_ROWS, 1), 0) + me * OWN_ROWS
    hots = []
    for k in range(n_chip):
        g = lax.rem(chip - k + n_chip, n_chip)
        goal = column
        for i in range(2 * W):
            begin = starts_ref[0, live_slot(g * 2 * W + i)] - i * TOK
            goal = goal + jnp.where(lax.div(column, TOK) == i, begin, 0)
        hots.append(jnp.where(position == goal, 1.0, 0.0).astype(jnp.bfloat16))

    def place(h, s):
        value = jnp.dot(hots[0], placed[0, h, s], preferred_element_type=jnp.float32)
        for k in range(1, n_chip):
            value += jnp.dot(hots[k], placed[k, h, s], preferred_element_type=jnp.float32)
        to = pl.ds(pl.multiple_of(s * cols + h * piece, 128), piece)
        out_ref[:, to] = value.astype(jnp.bfloat16)

    for (k, h, step), relays in zip(out_copies, out_relays):
        for j in range(1, n_chip):
            step[j].wait_recv()
            relays[j - 1].start()
        if k == n_chip - 1:
            place(h, me)
    for k, h, step in out_copies:
        step[0].wait_recv()
        if k == n_chip - 1:
            place(h, partner)
    for relays in out_relays:
        for copy in relays:
            copy.wait_recv()
    for h in range(PIECES):
        for j in range(1, n_chip):
            place(h, source(j))
            place(h, source(j) + 1 - 2 * core)

    for copy in wave_copies + wave_relays + first_copies + first_relays + tok_copies + tok_relays:
        copy.wait_send()
    for (k, h, step), relays in zip(out_copies, out_relays):
        for copy in step + relays:
            copy.wait_send()


def shards(
    waveforms,
    clip_lengths,
    block_starts,
    conv_first,
    bias_first,
    conv_second,
    bias_second,
    norm_gain,
    projector,
    proj_bias,
):
    basis, filters = spectral_tables()
    n_seq = lax.axis_size("seq")
    n_batch = lax.axis_size("batch")
    n_chip = n_seq // 2
    slots = waveforms.shape[1]
    cols = projector.shape[1]
    piece = cols // PIECES
    hops = 2 * n_chip - 1
    anywhere = pl.BlockSpec(memory_space=pl.ANY)
    vmem = pl.BlockSpec(memory_space=pltpu.VMEM)
    smem = pl.BlockSpec(memory_space=pltpu.SMEM)
    dma = pltpu.SemaphoreType.DMA
    bf16 = jnp.bfloat16
    out = pl.pallas_call(
        functools.partial(kernel, n_seq, n_batch, slots),
        out_shape=jax.ShapeDtypeStruct((OWN_ROWS, n_seq * cols), bf16),
        in_specs=[
            smem,
            smem,
            anywhere,
            anywhere,
            vmem,
            anywhere,
            vmem,
            vmem,
            anywhere,
            vmem,
            anywhere,
            vmem,
        ],
        out_specs=vmem,
        scratch_shapes=[
            pltpu.VMEM((n_seq * slots, SEGS, SEG), bf16),
            pltpu.VMEM((n_batch,) + conv_first.shape, bf16),
            pltpu.VMEM(conv_second.shape, bf16),
            pltpu.VMEM(projector.shape, bf16),
            pltpu.VMEM(basis.shape, bf16),
            pltpu.VMEM((2 * ROWS, 3 * WIDTH), bf16),
            pltpu.VMEM((ROWS, WIDTH), jnp.float32),
            pltpu.VMEM((n_seq, 2 * ROWS, HALF), bf16),
            pltpu.VMEM((n_chip, PIECES, n_seq, 2 * ROWS, piece), bf16),
            dma((5,)),
            dma((hops,)),
            dma((hops,)),
            dma((2 * n_batch - 2,)),
            dma((2 * n_batch - 2,)),
            dma((hops,)),
            dma((hops,)),
            dma((n_chip, PIECES, hops)),
            dma((n_chip, PIECES, hops)),
        ],
        compiler_params=pltpu.CompilerParams(
            collective_id=0, has_side_effects=True, vmem_limit_bytes=60 * 1024 * 1024
        ),
        name="encoder",
    )(
        clip_lengths,
        block_starts,
        waveforms.reshape(slots, SEGS, SEG),
        conv_first,
        bias_first.reshape(1, -1),
        conv_second,
        bias_second.reshape(1, -1),
        norm_gain.reshape(1, -1),
        projector,
        proj_bias.reshape(1, -1),
        basis,
        filters,
    )
    return out[None]


def solution(mesh):
    return jax.shard_map(
        shards,
        mesh=mesh,
        in_specs=(
            P("batch", "seq", None),
            P("batch", None),
            P("batch", None),
            P("batch", None),
            P(),
            P(),
            P(),
            P(),
            P(None, "seq"),
            P("seq"),
        ),
        out_specs=P("batch", "seq", None),
        check_vma=False,
    )
```

```python
import functools

import jax
import jax.numpy as jnp
import ml_dtypes
import numpy as np
from jax import lax
from jax.experimental import pallas as pl
from jax.experimental.pallas import tpu as pltpu
from jax.sharding import PartitionSpec as P

MEL = 128
WIDTH = 1280
HOP = 160
WINDOW = 400
BINS = 201
TOK = 24
OWN_ROWS = 192
W = 3
ROWS = W * TOK
HALF = WIDTH // 2
CHUNK = 256
SEGS = 25
SEG = 4 * HOP
PARTS = 4
MESH = pl.DeviceIdType.MESH
VMEM_MIB = 48


def hertz_to_mel(hertz):
    return np.where(
        hertz < 1000.0,
        hertz / (200.0 / 3.0),
        15.0 + np.log(np.maximum(hertz, 1.0) / 1000.0) / (np.log(6.4) / 27.0),
    )


def mel_to_hertz(mels):
    return np.where(
        mels < 15.0, mels * 200.0 / 3.0, 1000.0 * np.exp((mels - 15.0) * np.log(6.4) / 27.0)
    )


def spectral_tables():
    sample_rate = HOP * 100.0
    sample_index = np.arange(WINDOW)
    hann = 0.5 - 0.5 * np.cos(2.0 * np.pi * sample_index / WINDOW)
    angles = 2.0 * np.pi * np.outer(sample_index, np.arange(BINS)) / WINDOW
    basis = np.zeros((512, 512), np.float32)
    basis[:WINDOW, :BINS] = hann[:, None] * np.cos(angles)
    basis[:WINDOW, 256 : 256 + BINS] = -hann[:, None] * np.sin(angles)
    edges = mel_to_hertz(
        np.linspace(0.0, float(hertz_to_mel(np.array(sample_rate / 2.0))), MEL + 2)
    )
    bin_hertz = np.arange(BINS) * sample_rate / WINDOW
    rising = (bin_hertz[:, None] - edges[None, :-2]) / (edges[1:-1] - edges[:-2])[None, :]
    falling = (edges[None, 2:] - bin_hertz[:, None]) / (edges[2:] - edges[1:-1])[None, :]
    filters = np.zeros((256, MEL), np.float32)
    filters[:BINS] = (
        np.maximum(0.0, np.minimum(rising, falling)) * (2.0 / (edges[2:] - edges[:-2]))[None, :]
    )
    terms = []
    rest = basis
    for _ in range(3):
        term = rest.astype(ml_dtypes.bfloat16)
        terms.append(term)
        rest = rest - term.astype(np.float32)
    return jnp.asarray(np.stack(terms)), jnp.asarray(filters)


def gelu(x):
    return 0.5 * x * (1.0 + lax.erf(x * np.float32(np.sqrt(0.5))))


def shift_rows(x, by):
    rows = x.shape[0]
    moved = pltpu.roll(x, by % rows, axis=0)
    place = lax.broadcasted_iota(jnp.int32, (rows, 1), 0) % TOK
    edge = 0 if by == 1 else TOK - 1
    return jnp.where(place == edge, 0.0, moved)


def kernel(
    n_seq,
    n_batch,
    slots,
    lengths_hbm,
    starts_hbm,
    waves_hbm,
    first_hbm,
    bias1_hbm,
    second_hbm,
    bias2_hbm,
    gain_hbm,
    projector_hbm,
    pbias_hbm,
    basis_hbm,
    filters_hbm,
    out_ref,
    lengths_ref,
    starts_ref,
    pbias_ref,
    filters_ref,
    waves,
    first,
    second,
    projector,
    basis,
    conv_in,
    pooled,
    tokens,
    placed,
    bias1_ref,
    bias2_ref,
    gain_ref,
    extra,
    extra_bias,
    local_sem,
    wave_send,
    wave_recv,
    first_send,
    first_recv,
    tok_send,
    tok_recv,
    out_send,
    out_recv,
    extra_send,
    extra_recv,
):
    me = lax.axis_index("seq")
    row = lax.axis_index("batch")
    core = lax.rem(me, 2)
    chip = lax.div(me, 2)
    n_chip = n_seq // 2
    partner = chip * 2 + (1 - core)
    cols = projector.shape[1]
    n_pieces, n_far, piece = split(n_chip, cols)

    def across(k):
        return lax.rem(chip + k, n_chip) * 2 + core

    def source(k):
        return lax.rem(chip - k + n_chip, n_chip) * 2 + core

    def peer(k):
        return lax.rem(row + k, n_batch)

    loads = [
        pltpu.make_async_copy(waves_hbm, waves.at[me], local_sem.at[0]),
        pltpu.make_async_copy(basis_hbm, basis, local_sem.at[1]),
        pltpu.make_async_copy(first_hbm, first.at[row], local_sem.at[2]),
        pltpu.make_async_copy(second_hbm, second, local_sem.at[3]),
        pltpu.make_async_copy(projector_hbm, projector, local_sem.at[4]),
        pltpu.make_async_copy(bias1_hbm, bias1_ref.at[0], local_sem.at[5]),
        pltpu.make_async_copy(bias2_hbm, bias2_ref.at[0], local_sem.at[6]),
        pltpu.make_async_copy(gain_hbm, gain_ref.at[0], local_sem.at[7]),
        pltpu.make_async_copy(pbias_hbm, pbias_ref.at[0], local_sem.at[8]),
        pltpu.make_async_copy(filters_hbm, filters_ref, local_sem.at[9]),
        pltpu.make_async_copy(lengths_hbm, lengths_ref, local_sem.at[10]),
        pltpu.make_async_copy(starts_hbm, starts_ref, local_sem.at[11]),
    ]
    for load in loads[:1] + loads[2:3] + loads[1:2] + loads[5:] + loads[3:5]:
        load.start()

    barrier = pltpu.get_barrier_semaphore()
    pl.semaphore_signal(barrier, inc=1, device_id=(partner, row), device_id_type=MESH)
    for k in range(1, n_chip):
        pl.semaphore_signal(barrier, inc=1, device_id=(across(k), row), device_id_type=MESH)
    for k in range(1, n_batch):
        pl.semaphore_signal(barrier, inc=1, device_id=(me, peer(k)), device_id_type=MESH)
    pl.semaphore_wait(barrier, n_chip + n_batch - 1)

    def gather(own, place, send, recv):
        copies = []
        for k in range(n_chip):
            target = partner if k == 0 else across(k)
            copies.append(
                pltpu.make_async_remote_copy(
                    src_ref=own,
                    dst_ref=place(me),
                    send_sem=send.at[k],
                    recv_sem=recv.at[k],
                    device_id=(target, row),
                    device_id_type=MESH,
                )
            )
        return copies

    def relay(place, send, recv):
        return [
            pltpu.make_async_remote_copy(
                src_ref=place(source(k)),
                dst_ref=place(source(k)),
                send_sem=send.at[n_chip - 1 + k],
                recv_sem=recv.at[n_chip - 1 + k],
                device_id=(partner, row),
                device_id_type=MESH,
            )
            for k in range(1, n_chip)
        ]

    def wave_place(s):
        return waves.at[s]

    wave_copies = gather(waves_hbm, wave_place, wave_send, wave_recv)
    wave_relays = relay(wave_place, wave_send, wave_recv)
    for copy in wave_copies[1:] + wave_copies[:1]:
        copy.start()

    half = pl.ds(pl.multiple_of(core * HALF, 128), HALF)
    first_copies = []
    first_relays = []
    for k in range(1, n_batch):
        first_copies.append(
            pltpu.make_async_remote_copy(
                src_ref=first_hbm.at[:, half],
                dst_ref=first.at[row, :, half],
                send_sem=first_send.at[k - 1],
                recv_sem=first_recv.at[k - 1],
                device_id=(me, peer(k)),
                device_id_type=MESH,
            )
        )
        origin = lax.rem(row - k + n_batch, n_batch)
        first_relays.append(
            pltpu.make_async_remote_copy(
                src_ref=first.at[origin, :, half],
                dst_ref=first.at[origin, :, half],
                send_sem=first_send.at[n_batch - 2 + k],
                recv_sem=first_recv.at[n_batch - 2 + k],
                device_id=(partner, row),
                device_id_type=MESH,
            )
        )
    for copy in first_copies:
        copy.start()

    lane = lax.rem(row, 2)
    beside = row + 1 - 2 * lane
    part = WIDTH // PARTS
    extra_copies = []
    extra_relays = []
    if n_far < n_pieces:
        from_col = pl.multiple_of((n_far + lane) * piece, 128)
        for i in range(PARTS):
            at = pl.ds(i * part, part)
            extra_copies.append(
                pltpu.make_async_remote_copy(
                    src_ref=projector_hbm.at[at, pl.ds(from_col, piece)],
                    dst_ref=extra.at[lane, at],
                    send_sem=extra_send.at[i],
                    recv_sem=extra_recv.at[i],
                    device_id=(across(1), row),
                    device_id_type=MESH,
                )
            )
            extra_relays.append(
                pltpu.make_async_remote_copy(
                    src_ref=extra.at[lane, at],
                    dst_ref=extra.at[lane, at],
                    send_sem=extra_send.at[PARTS + i],
                    recv_sem=extra_recv.at[PARTS + i],
                    device_id=(me, beside),
                    device_id_type=MESH,
                )
            )
        extra_copies.append(
            pltpu.make_async_remote_copy(
                src_ref=pbias_hbm,
                dst_ref=extra_bias.at[0],
                send_sem=extra_send.at[2 * PARTS],
                recv_sem=extra_recv.at[2 * PARTS],
                device_id=(across(1), row),
                device_id_type=MESH,
            )
        )
        for copy in extra_copies:
            copy.start()

    def pass_on(i):
        if extra_relays:
            extra_copies[i].wait_recv()
            extra_relays[i].start()

    for k in range(1, n_chip):
        wave_copies[k].wait_recv()
        wave_relays[k - 1].start()
    wave_copies[0].wait_recv()
    for copy in wave_relays:
        copy.wait_recv()
    loads[0].wait()
    for load in loads[9:]:
        load.wait()

    ends = []
    total = 0
    for d in range(n_seq):
        total = total + lengths_ref[0, d]
        ends.append(total)

    def live_slot(j):
        device, slot = 0, j
        for d in range(n_seq - 1):
            past = j >= ends[d]
            device = device + jnp.where(past, 1, 0)
            slot = slot - jnp.where(past, lengths_ref[0, d], 0)
        return device, jnp.clip(slot, 0, slots - 1)

    pieces = []
    for i in range(W):
        device, slot = live_slot(me * W + i)
        clip = waves[device].astype(jnp.float32)
        mine = lax.broadcasted_iota(jnp.int32, (slots, 1), 0) == slot
        line = jnp.sum(jnp.where(mine, clip, 0.0), axis=0, keepdims=True)
        block = jnp.concatenate(
            [line[:, q * SEG : (q + 1) * SEG] for q in range(SEGS)], axis=0
        )
        pieces.append(jnp.concatenate([block[: SEGS - 1], block[1:, :256]], axis=1))
    samples = jnp.concatenate(pieces, axis=0)
    frames = [samples[:, :512]]
    for r in range(1, 4):
        wide = samples[:, 128 * r : min(128 * r + 640, 896)]
        frames.append(pltpu.roll(wide, wide.shape[1] - 32 * r, axis=1)[:, :512])
    frames = jnp.concatenate(frames, axis=0).astype(jnp.bfloat16)
    loads[1].wait()
    spectrum = jnp.dot(frames, basis[2], preferred_element_type=jnp.float32)
    spectrum += jnp.dot(frames, basis[1], preferred_element_type=jnp.float32)
    spectrum += jnp.dot(frames, basis[0], preferred_element_type=jnp.float32)
    real, imag = spectrum[:, :256], spectrum[:, 256:]
    power = real * real + imag * imag
    energy = jnp.dot(
        power,
        filters_ref[...],
        precision=lax.Precision.HIGHEST,
        preferred_element_type=jnp.float32,
    )
    features = (jnp.log(energy + 1e-10) * np.float32(1.0 / np.log(10.0)) + 4.0) * 0.25
    feat = [features[r * ROWS : (r + 1) * ROWS] for r in range(4)]
    stacked = jnp.concatenate(
        [
            jnp.concatenate([shift_rows(feat[3], 1)] + feat[:3], axis=0),
            features,
            jnp.concatenate(feat[1:] + [shift_rows(feat[0], -1)], axis=0),
        ],
        axis=1,
    ).astype(jnp.bfloat16)

    for k in range(n_batch - 1):
        first_copies[k].wait_recv()
        first_relays[k].start()
    loads[2].wait()
    loads[5].wait()
    pass_on(0)

    def first_half(begin):
        at = pl.ds(pl.multiple_of(begin, 128), HALF)
        weight = first[:, :, at].reshape(3 * MEL, HALF)
        hidden = gelu(
            jnp.dot(stacked, weight, preferred_element_type=jnp.float32) + bias1_ref[:, at]
        )
        hid = [hidden[r * ROWS : (r + 1) * ROWS] for r in range(4)]
        taps = [[shift_rows(hid[3], 1), hid[1]], [hid[0], hid[2]], [hid[1], hid[3]]]
        for t in range(3):
            to = pl.ds(pl.multiple_of(t * WIDTH + begin, 128), HALF)
            conv_in[:, to] = jnp.concatenate(taps[t], axis=0).astype(jnp.bfloat16)

    first_half(core * HALF)
    for copy in first_relays:
        copy.wait_recv()
    first_half((1 - core) * HALF)
    pass_on(1)

    loads[6].wait()
    loads[7].wait()
    loads[3].wait()

    @pl.loop(0, WIDTH // CHUNK)
    def _(n):
        at = pl.ds(pl.multiple_of(n * CHUNK, CHUNK), CHUNK)
        activated = gelu(
            jnp.dot(conv_in[...], second[:, at], preferred_element_type=jnp.float32)
            + bias2_ref[:, at]
        )
        pooled[:, at] = (activated[:ROWS] + activated[ROWS:]) * 0.5

    pass_on(2)
    whole = pooled[...]
    centred = whole - jnp.mean(whole, axis=1, keepdims=True)
    variance = jnp.mean(centred * centred, axis=1, keepdims=True)
    normed = centred / jnp.sqrt(variance + 1e-05) * gain_ref[...]
    tokens[me] = jnp.concatenate([normed[:, :HALF], normed[:, HALF:]], axis=0).astype(jnp.bfloat16)

    def tok_place(s):
        return tokens.at[s]

    tok_copies = gather(tokens.at[me], tok_place, tok_send, tok_recv)
    tok_relays = relay(tok_place, tok_send, tok_recv)
    for copy in tok_copies[1:] + tok_copies[:1]:
        copy.start()
    pass_on(3)
    tok_copies[0].wait_recv()
    loads[4].wait()
    loads[8].wait()

    def group_rows(g):
        pair = [tokens[g * 2 + c].astype(jnp.float32) for c in range(2)]
        left = jnp.concatenate([p[:ROWS] for p in pair], axis=0).astype(jnp.bfloat16)
        right = jnp.concatenate([p[ROWS:] for p in pair], axis=0).astype(jnp.bfloat16)
        return left, right

    def project(rows, weight, bias):
        value = jnp.dot(rows[0], weight[:HALF], preferred_element_type=jnp.float32)
        value += jnp.dot(rows[1], weight[HALF:], preferred_element_type=jnp.float32)
        return (value + bias).astype(jnp.bfloat16)

    def far_slot(k, j):
        return (k + j) % n_chip

    steps = {}
    relays = {}
    for k in range(n_chip):
        for h in range(n_pieces):
            steps[k, h] = [
                pltpu.make_async_remote_copy(
                    src_ref=placed.at[k, h, me],
                    dst_ref=placed.at[far_slot(k, j), h, me],
                    send_sem=out_send.at[k, h, j],
                    recv_sem=out_recv.at[k, h, j],
                    device_id=(partner if j == 0 else across(j), row),
                    device_id_type=MESH,
                )
                for j in range(n_chip if h < n_far else 1)
            ]
            relays[k, h] = [
                pltpu.make_async_remote_copy(
                    src_ref=placed.at[far_slot(k, j), h, source(j)],
                    dst_ref=placed.at[far_slot(k, j), h, source(j)],
                    send_sem=out_send.at[k, h, n_chip - 1 + j],
                    recv_sem=out_recv.at[k, h, n_chip - 1 + j],
                    device_id=(partner, row),
                    device_id_type=MESH,
                )
                for j in range(1, n_chip)
            ]

    def own_piece(k, h, rows):
        at = slice(h * piece, (h + 1) * piece)
        placed[k, h, me] = project(rows, projector[:, at], pbias_ref[:, at])
        for copy in steps[k, h][1:] + steps[k, h][:1]:
            copy.start()

    grouped = []
    for k in range(n_chip):
        g = lax.rem(chip - k + n_chip, n_chip)
        if k > 0:
            tok_copies[k].wait_recv()
            tok_relays[k - 1].start()
            tok_relays[k - 1].wait_recv()
        grouped.append(group_rows(g))
        for h in range(n_far):
            own_piece(k, h, grouped[k])
    for k in range(n_chip):
        for h in range(n_far, n_pieces):
            own_piece(k, h, grouped[k])
    if extra_relays:
        extra_copies[PARTS].wait_recv()
        for copy in extra_relays:
            copy.wait_recv()
        for k in range(n_chip):
            for h in range(n_far, n_pieces):
                at = slice(h * piece, (h + 1) * piece)
                to = far_slot(k, 1)
                placed[to, h, source(1)] = project(
                    grouped[to], extra[h - n_far], extra_bias[:, at]
                )
                relays[k, h][0].start()

    span = 2 * ROWS
    column = lax.broadcasted_iota(jnp.int32, (1, span), 1)
    position = lax.broadcasted_iota(jnp.int32, (OWN_ROWS, 1), 0) + me * OWN_ROWS
    hots = []
    for k in range(n_chip):
        g = lax.rem(chip - k + n_chip, n_chip)
        goal = column
        for i in range(2 * W):
            device, slot = live_slot(g * 2 * W + i)
            begin = starts_ref[0, device * slots + slot] - i * TOK
            goal = goal + jnp.where(lax.div(column, TOK) == i, begin, 0)
        hots.append(jnp.where(position == goal, 1.0, 0.0).astype(jnp.bfloat16))

    def place(h, s):
        value = jnp.dot(hots[0], placed[0, h, s], preferred_element_type=jnp.float32)
        for k in range(1, n_chip):
            value += jnp.dot(hots[k], placed[k, h, s], preferred_element_type=jnp.float32)
        to = pl.ds(pl.multiple_of(s * cols + h * piece, 128), piece)
        out_ref[:, to] = value.astype(jnp.bfloat16)

    for h in range(n_pieces):
        place(h, me)
    for k in range(n_chip):
        for h in range(n_pieces):
            steps[k, h][0].wait_recv()
    for h in range(n_pieces):
        place(h, partner)
    for k in range(n_chip):
        for h in range(n_far):
            for j in range(1, n_chip):
                steps[k, h][j].wait_recv()
                relays[k, h][j - 1].start()
    for h in reversed(range(n_pieces)):
        for j in range(1, n_chip):
            place(h, source(j))
    for k in range(n_chip):
        for h in range(n_pieces):
            for copy in relays[k, h]:
                copy.wait_recv()
    for h in range(n_pieces):
        for j in range(1, n_chip):
            place(h, source(j) + 1 - 2 * core)

    for copy in wave_copies + wave_relays + first_copies + first_relays + tok_copies + tok_relays:
        copy.wait_send()
    for copy in extra_copies + extra_relays:
        copy.wait_send()
    for key in steps:
        for copy in steps[key]:
            copy.wait_send()
        for copy in relays[key]:
            copy.wait_send()


def split(n_chip, cols):
    if n_chip == 2 and cols % 512 == 0:
        return 4, 2, cols // 4
    return 2, 2, cols // 2


def shards(
    waveforms,
    clip_lengths,
    block_starts,
    conv_first,
    bias_first,
    conv_second,
    bias_second,
    norm_gain,
    projector,
    proj_bias,
):
    basis, filters = spectral_tables()
    n_seq = lax.axis_size("seq")
    n_batch = lax.axis_size("batch")
    n_chip = n_seq // 2
    slots = waveforms.shape[1]
    cols = projector.shape[1]
    n_pieces, _, piece = split(n_chip, cols)
    hops = 2 * n_chip - 1
    hbm = pl.BlockSpec(memory_space=pltpu.HBM)
    vmem = pl.BlockSpec(memory_space=pltpu.VMEM)
    dma = pltpu.SemaphoreType.DMA
    bf16 = jnp.bfloat16
    out = pl.pallas_call(
        functools.partial(kernel, n_seq, n_batch, slots),
        out_shape=jax.ShapeDtypeStruct((OWN_ROWS, n_seq * cols), bf16),
        in_specs=[hbm] * 12,
        out_specs=vmem,
        scratch_shapes=[
            pltpu.SMEM(clip_lengths.shape, jnp.int32),
            pltpu.SMEM(block_starts.shape, jnp.int32),
            pltpu.VMEM((1, cols), jnp.float32),
            pltpu.VMEM(filters.shape, jnp.float32),
            pltpu.VMEM((n_seq, slots, SEGS * SEG), bf16),
            pltpu.VMEM((n_batch,) + conv_first.shape, bf16),
            pltpu.VMEM(conv_second.shape, bf16),
            pltpu.VMEM(projector.shape, bf16),
            pltpu.VMEM(basis.shape, bf16),
            pltpu.VMEM((2 * ROWS, 3 * WIDTH), bf16),
            pltpu.VMEM((ROWS, WIDTH), jnp.float32),
            pltpu.VMEM((n_seq, 2 * ROWS, HALF), bf16),
            pltpu.VMEM((n_chip, n_pieces, n_seq, 2 * ROWS, piece), bf16),
            pltpu.VMEM((1, WIDTH), jnp.float32),
            pltpu.VMEM((1, WIDTH), jnp.float32),
            pltpu.VMEM((1, WIDTH), jnp.float32),
            pltpu.VMEM((2, WIDTH, piece), bf16),
            pltpu.VMEM((1, cols), jnp.float32),
            dma((12,)),
            dma((hops,)),
            dma((hops,)),
            dma((2 * n_batch - 2,)),
            dma((2 * n_batch - 2,)),
            dma((hops,)),
            dma((hops,)),
            dma((n_chip, n_pieces, hops)),
            dma((n_chip, n_pieces, hops)),
            dma((2 * PARTS + 1,)),
            dma((2 * PARTS + 1,)),
        ],
        compiler_params=pltpu.CompilerParams(
            collective_id=0, has_side_effects=True, vmem_limit_bytes=VMEM_MIB * 1024 * 1024
        ),
        name="encoder",
    )(
        *[
            pltpu.with_memory_space_constraint(x, pltpu.HBM)
            for x in (
                clip_lengths,
                block_starts,
                waveforms.reshape(slots, SEGS * SEG),
                conv_first,
                bias_first,
                conv_second,
                bias_second,
                norm_gain,
                projector,
                proj_bias,
                basis,
                filters,
            )
        ]
    )
    return out[None]


def solution(mesh):
    return jax.shard_map(
        shards,
        mesh=mesh,
        in_specs=(
            P("batch", "seq", None),
            P("batch", None),
            P("batch", None),
            P("batch", None),
            P(),
            P(),
            P(),
            P(),
            P(None, "seq"),
            P("seq"),
        ),
        out_specs=P("batch", "seq", None),
        check_vma=False,
    )
```
